256 devices in a mesh: state: 16 (over y_lo, x, core), mesh: 16 (over z, y_hi).
Axes of the slice: x: 4, y: 4 (y_hi: 2, y_lo: 2; y = y_hi * 2 + y_lo), z: 8, core: 2. Of those that a mesh axis runs over, the one named last changes fastest.
Arguments:
- states_in: float32 [22032, 4096], P('mesh', 'state'), may hold values from -6 to 6
- rotation: float32 [4096, 4096], P(None, 'state'), may hold values from -0.09375 to 0.09375
- stiffness: float32 [16, 729, 729], P('mesh'), as said below
- potential: float32 [22032], P('mesh'), may hold values from -1 to 1
- cell_nodes: int32 [32, 729], P('mesh'), may hold values from 0 to 1376, as said below
- shared_rows: int32 [64, 153], P('mesh'), may hold values from 0 to 1376, as said below
- shared_count: int32 [16, 4], P('mesh'), may hold values from 0 to 153, as said below
Outputs:
- filtered: float32 [22032, 4096], P('mesh', 'state')
The draws below stay inside these ranges and needn't reach their ends.
Inputs may be any that keep to these rules, and one draw needn't show every extreme that they name: `cell_nodes`: each partition's 2 cells name its 1377 local nodes as a row of hexahedral cells of order 8 sharing faces; every local node is named by some cell. `shared_rows`: used rows name the partition's nodes on the face toward the partner, in the same geometric order as the partner's matching list; rows beyond the count name arbitrary local nodes. `shared_count`: count s of partition p equals count s ^ 1 of its partner; for s = 0, 1 it is 0 or from 40 to 81, for s = 2, 3 it is 0 or from 76 to 153; it is 0 where the partner lies outside the G by G grid; count 2 of partition 0 is 153. `stiffness`: symmetric with a diagonal of 1 to 3.
All inputs are finite; a program needn't handle non-finite values.
Results may differ from the reference program's by a relative error of at most 0.0001.
Values sent between devices are 32-bit elements; how exact they have to be, the bound alone decides.
No kernel may reach another device: no remote copies, remote signals or barrier semaphores. Data moves between devices by JAX's collectives and lax.ppermute only.
A program may use at most 64 MiB of HBM per device.

```python
import math
import jax
import jax.numpy as jnp
from jax import lax

NSTATE = 4096
ORDER = 8
CELLS = 2
CHEB = 2
NPC = 729
NODE_DEV = 1377
FACE_X = 81
SHARE_MAX = 153
NODES = 22032
N_MESH = 16


def mesh_layout(key):
    side = ORDER + 1
    grid_side = math.isqrt(N_MESH)
    keys = jax.random.split(jax.random.fold_in(key, 11), N_MESH)
    perms = jax.vmap(lambda sub: jax.random.permutation(sub, NODE_DEV))(keys).astype(jnp.int32)
    local = jnp.arange(NPC, dtype=jnp.int32)
    first = local // (side * side)
    second = local // side % side
    third = local % side
    cellidx = jnp.arange(CELLS, dtype=jnp.int32)[:, None]
    structure = ((cellidx * ORDER + first[None, :]) * side + second[None, :]) * side + third[None, :]
    nodes = perms[:, structure].reshape(N_MESH * CELLS, NPC)
    face_rows = jnp.arange(FACE_X, dtype=jnp.int32)
    far_x = CELLS * ORDER
    face_high = (far_x * side + face_rows // side) * side + face_rows % side
    face_low = face_rows // side * side + face_rows % side
    pad = jnp.zeros((SHARE_MAX - FACE_X,), jnp.int32)
    face_high = jnp.concatenate([face_high, pad])
    face_low = jnp.concatenate([face_low, pad])
    long_rows = jnp.arange(SHARE_MAX, dtype=jnp.int32)
    side_high = (long_rows // side * side + ORDER) * side + long_rows % side
    side_low = long_rows // side * side * side + long_rows % side
    lists = jnp.stack([face_high, face_low, side_high, side_low])
    rows = perms[:, lists].reshape(N_MESH * 4, SHARE_MAX)
    parts = jnp.arange(N_MESH, dtype=jnp.int32)
    place_a = parts // grid_side
    place_b = parts % grid_side
    link_a = jax.random.randint(jax.random.fold_in(key, 23), (N_MESH,), 0, 4) < 3
    link_b = jax.random.randint(jax.random.fold_in(key, 29), (N_MESH,), 0, 4) < 3
    link_b = link_b | (parts == 0)
    size_a = jax.random.randint(jax.random.fold_in(key, 31), (N_MESH,), FACE_X // 2, FACE_X + 1)
    size_b = jax.random.randint(jax.random.fold_in(key, 43), (N_MESH,), SHARE_MAX // 2, SHARE_MAX + 1)
    size_b = jnp.where(parts == 0, SHARE_MAX, size_b)
    count_zero = jnp.where((place_a < grid_side - 1) & link_a, size_a, 0)
    count_two = jnp.where((place_b < grid_side - 1) & link_b, size_b, 0)
    count_one = jnp.roll(count_zero, grid_side)
    count_one = jnp.where(place_a > 0, count_one, 0)
    count_three = jnp.roll(count_two, 1)
    count_three = jnp.where(place_b > 0, count_three, 0)
    counts = jnp.stack([count_zero, count_one, count_two, count_three], axis=1).astype(jnp.int32)
    return (nodes, rows, counts)


def draw_cell_nodes(key, part):
    return mesh_layout(key)[0]


def draw_shared_rows(key, part):
    return mesh_layout(key)[1]


def draw_shared_count(key, part):
    return mesh_layout(key)[2]


def draw_stiffness(key, part):
    inner = jax.random.fold_in(key, 37)
    raw = jax.random.normal(inner, (N_MESH, NPC, NPC), jnp.float32)
    offdiag = (raw + jnp.swapaxes(raw, 1, 2)) * (0.7 / math.sqrt(NPC))
    diag_vals = jax.random.uniform(jax.random.fold_in(key, 41), (N_MESH, NPC), jnp.float32, 1.0, 3.0)
    unit = jnp.eye(NPC, dtype=jnp.float32)
    return offdiag * (1.0 - unit)[None] + unit[None] * diag_vals[:, :, None]


def block_levels(stream_key, extent, shards, low, high):
    loudness = 1.0
    for dim, blocks in shards:
        heights = jax.random.uniform(jax.random.fold_in(jax.random.fold_in(stream_key, 6), dim), (blocks,), jnp.float32, low / len(shards), high / len(shards))
        loudness = loudness * jnp.repeat(jnp.exp(heights), extent[dim] // blocks).reshape((-1,) + (1,) * (len(extent) - 1 - dim))
    return loudness


def bell_draw(key, dims, spread, most, pieces=(), kind=jnp.bfloat16):
    array = jax.random.normal(key, dims, jnp.float32) * spread
    if len(pieces) > 0:
        array = block_levels(key, dims, pieces, -0.22, 0.18) * array
    return jnp.clip(array, min=-most, max=most).astype(kind)


def setup_inputs(seed: int = 0) -> dict:
    key_of = jax.random.split(jax.random.key(seed), 8)
    return {
        "states_in": bell_draw(key_of[0], (NODES, NSTATE), 1.0, 6.0, ((0, 16), (1, 16)), jnp.float32),
        "rotation": bell_draw(key_of[1], (NSTATE, NSTATE), NSTATE ** -0.5, 0.09375, ((1, 16),), jnp.float32),
        "stiffness": draw_stiffness(jax.random.fold_in(key_of[7], 71), 0),
        "potential": jnp.clip(jax.random.uniform(key_of[3], (NODES,), jnp.float32, -1.0, 1.0) * block_levels(key_of[3], (NODES,), ((0, 16),), -0.4, 0.0), -1.0, 1.0),
        "cell_nodes": draw_cell_nodes(jax.random.fold_in(key_of[7], 71), 0),
        "shared_rows": draw_shared_rows(jax.random.fold_in(key_of[7], 71), 0),
        "shared_count": draw_shared_count(jax.random.fold_in(key_of[7], 71), 0),
    }


center_shift = 3.0
half_width = 4.0

def apply_cells(field, stiffness, nodes):

    def single(packed):
        values, matrix, index = packed
        gathered = values[index]
        product = jnp.einsum('ij,cjs->cis', matrix, gathered, precision=lax.Precision.HIGHEST)
        return jnp.zeros_like(values).at[index.reshape(-1)].add(product.reshape(-1, values.shape[1]))
    return lax.map(single, (field, stiffness, nodes))

def pick_rows(values, rows, mask, slot):
    return jax.vmap(lambda vals, idx, msk: vals[idx[slot]] * msk[slot][:, None])(values, rows, mask)

def put_rows(values, rows, slot, got):
    return jax.vmap(lambda vals, idx, add: vals.at[idx[slot]].add(add))(values, rows, got)

def operator(field, stiffness, potential, nodes, rows, mask, grid_side):
    local = apply_cells(field, stiffness, nodes)
    send_one = pick_rows(local, rows, mask, 1)
    send_zero = pick_rows(local, rows, mask, 0)
    from_next = jnp.roll(send_one, -grid_side, axis=0) * mask[:, 0, :, None]
    from_prev = jnp.roll(send_zero, grid_side, axis=0) * mask[:, 1, :, None]
    sectioned = put_rows(put_rows(local, rows, 0, from_next), rows, 1, from_prev)
    send_three = pick_rows(sectioned, rows, mask, 3)
    send_two = pick_rows(sectioned, rows, mask, 2)
    from_right = jnp.roll(send_three, -1, axis=0) * mask[:, 2, :, None]
    from_left = jnp.roll(send_two, 1, axis=0) * mask[:, 3, :, None]
    assembled = put_rows(put_rows(sectioned, rows, 2, from_right), rows, 3, from_left)
    return assembled + potential[:, :, None] * field

def reference(states_in, rotation, stiffness, potential, cell_nodes, shared_rows, shared_count):
    rotated = jnp.dot(states_in, rotation, precision=lax.Precision.HIGHEST, preferred_element_type=jnp.float32)
    grid_side = math.isqrt(N_MESH)
    field = rotated.reshape(N_MESH, NODE_DEV, NSTATE)
    pot = potential.reshape(N_MESH, NODE_DEV)
    nodes = cell_nodes.reshape(N_MESH, CELLS, NPC)
    rows = shared_rows.reshape(N_MESH, 4, SHARE_MAX)
    mask = (jnp.arange(SHARE_MAX)[None, None, :] < shared_count[:, :, None]).astype(jnp.float32)
    previous = field
    current = (operator(field, stiffness, pot, nodes, rows, mask, grid_side) - center_shift * field) / half_width
    for step_index in range(1, CHEB):
        applied = operator(current, stiffness, pot, nodes, rows, mask, grid_side)
        following = 2.0 * (applied - center_shift * current) / half_width - previous
        previous = current
        current = following
    return current.reshape(NODES, NSTATE)
```

```python
import math

import jax
import jax.numpy as jnp
from jax import lax
from jax.sharding import PartitionSpec as P

center_shift = 3.0
half_width = 4.0
SIDE_X = 4
SIDE_Y = 2


def state_id(y, x, core):
    return (y % SIDE_Y) * (SIDE_X * 2) + (x % SIDE_X) * 2 + core % 2


def shift_state(value, dy, dx, dcore):
    pairs = [
        (state_id(y, x, c), state_id(y + dy, x + dx, c + dcore))
        for y in range(SIDE_Y)
        for x in range(SIDE_X)
        for c in range(2)
    ]
    return lax.ppermute(value, "state", pairs)


def shift_mesh(value, steps):
    count = lax.axis_size("mesh")
    first, last = (max(0, -steps), min(count, count - steps))
    return lax.ppermute(value, "mesh", [(source, source + steps) for source in range(first, last)])


def matmul(left, right):
    return jnp.dot(left, right, precision=lax.Precision.HIGH, preferred_element_type=jnp.float32)


def rotate(block, rotation):
    rows, cols = block.shape
    own = lax.axis_index("state")
    y, x, core = own // (SIDE_X * 2), (own // 2) % SIDE_X, own % 2
    chips = rotation.reshape(SIDE_Y * SIDE_X, 2, cols, cols)
    theirs = lax.dynamic_index_in_dim(chips, 1 - core, 1, keepdims=False)
    partner = shift_state(theirs, 0, 0, 1)
    half = rows // 16 * 8

    left = shift_state(block, 0, 1, 0)
    right = shift_state(block, 0, -1, 0)
    across = shift_state(block, 1, 0, 0)
    far_top = shift_state(left[:half], 0, 1, 0)
    far_low = shift_state(right[half:], 0, -1, 0)
    across_left = shift_state(across, 0, 1, 0)
    across_right = shift_state(across, 0, -1, 0)
    across_far_top = shift_state(far_top, 1, 0, 0)
    across_far_low = shift_state(far_low, 1, 0, 0)

    def part(value, dy, dx):
        chip = ((y + dy) % SIDE_Y) * SIDE_X + (x + dx) % SIDE_X
        mine = lax.dynamic_slice_in_dim(rotation, (chip * 2 + core) * cols, cols, 0)
        other = lax.dynamic_index_in_dim(partner, chip, 0, keepdims=False)
        return matmul(value, mine), matmul(value, other)

    def add(a, b):
        return a[0] + b[0], a[1] + b[1]

    total = part(block, 0, 0)
    total = add(total, part(left, 0, -1))
    total = add(total, part(right, 0, 1))
    total = add(total, part(across, 1, 0))
    total = add(total, part(jnp.concatenate([far_top, far_low]), 0, 2))
    total = add(total, part(across_left, 1, -1))
    total = add(total, part(across_right, 1, 1))
    total = add(total, part(jnp.concatenate([across_far_top, across_far_low]), 1, 2))
    return total[0] + shift_state(total[1], 0, 0, 1)


def per_device(states_in, rotation, stiffness, potential, cell_nodes, shared_rows, shared_count):
    block_cols = states_in.shape[1]
    rotated = rotate(states_in, rotation)
    grid_side = math.isqrt(lax.axis_size("mesh"))
    row_mask = (jnp.arange(shared_rows.shape[1])[None, :] < shared_count[0][:, None]).astype(
        jnp.float32
    )

    def trade(values, send_slot, recv_slot, offset):
        block = values[shared_rows[send_slot]] * row_mask[send_slot][:, None]
        arrived = shift_mesh(block, offset)
        return arrived * row_mask[recv_slot][:, None]

    def operator(field):
        gathered = field[cell_nodes]
        product = jnp.einsum("ij,cjs->cis", stiffness[0], gathered, precision=lax.Precision.HIGH)
        local = (
            jnp.zeros_like(field).at[cell_nodes.reshape(-1)].add(product.reshape(-1, block_cols))
        )
        from_next = trade(local, 1, 0, -grid_side)
        from_prev = trade(local, 0, 1, grid_side)
        sectioned = local.at[shared_rows[0]].add(from_next).at[shared_rows[1]].add(from_prev)
        from_right = trade(sectioned, 3, 2, -1)
        from_left = trade(sectioned, 2, 3, 1)
        assembled = sectioned.at[shared_rows[2]].add(from_right).at[shared_rows[3]].add(from_left)
        return assembled + potential[:, None] * field

    current = (operator(rotated) - center_shift * rotated) / half_width
    applied = operator(current)
    following = 2.0 * (applied - center_shift * current) / half_width - rotated
    return following


def solution(mesh):
    return jax.shard_map(
        per_device,
        mesh=mesh,
        in_specs=(
            P("mesh", "state"),
            P(None, "state"),
            P("mesh", None, None),
            P("mesh"),
            P("mesh", None),
            P("mesh", None),
            P("mesh", None),
        ),
        out_specs=P("mesh", "state"),
        check_vma=False,
    )
```

```python
import functools
import math

import jax
import jax.numpy as jnp
from jax import lax
from jax.experimental import pallas as pl
from jax.experimental.pallas import tpu as pltpu
from jax.sharding import PartitionSpec as P

center_shift = 3.0
half_width = 4.0
SIDE_X = 4
SIDE_Y = 2
LANES = 128
NEAR = 81


def up(value, unit):
    return -(-value // unit) * unit


def halves(value):
    high = value.astype(jnp.bfloat16)
    low = (value - high.astype(jnp.float32)).astype(jnp.bfloat16)
    return high, low


def pair(value):
    return jnp.concatenate(halves(value), axis=-1)


def dot(left, right):
    return jnp.dot(left, right, preferred_element_type=jnp.float32)


def fold(value):
    cols = value.shape[-1] // 2
    return value[..., :cols] + value[..., cols:]


def select(table, both):
    return fold(dot(table, both))


def cell_product(k_high, k_low, both, cols):
    return fold(dot(k_high, both)) + dot(k_low, both[:, :cols])


def cells_apply(both, k_high, k_low, c01, c10, m01, local_ref, send_ref):
    pad = k_high.shape[0]
    cols = both.shape[-1] // 2
    first = cell_product(k_high, k_low, both[:pad], cols)
    second = cell_product(k_high, k_low, both[pad:], cols)
    p_first, p_second = pair(first), pair(second)
    local_ref[:pad] = first + select(c01, p_second)
    local_ref[pad:] = second + select(c10, p_first)
    send = select(m01[:, :pad], p_first) + select(m01[:, pad:], p_second)
    send_ref[...] = send.reshape(send_ref.shape)


def enter_kernel(v, gather, k_high, k_low, c01, c10, m01, field, local, send, held):
    rows, cols = v.shape
    held[...] = jnp.zeros_like(held)
    high, low = halves(v[...])
    held[:rows, :cols] = high
    held[:rows, cols:] = low
    got = dot(gather[...], held[...])
    field[...] = fold(got)
    cells_apply(
        got.astype(jnp.bfloat16), k_high[...], k_low[...], c01[...], c10[...], m01[...], local, send
    )


def middle_kernel(local, recv, m01t, m23, sectioned, send):
    got = jnp.concatenate([recv[0], recv[1]], axis=0)
    value = local[...] + select(m01t[...], pair(got))
    sectioned[...] = value
    out = select(m23[...], pair(value))
    send[...] = out.reshape(send.shape)


def again_kernel(
    sectioned, recv, m23t, pot, field, k_high, k_low, c01, c10, m01, current, local, send
):
    got = jnp.concatenate([recv[0], recv[1]], axis=0)
    value = sectioned[...] + select(m23t[...], pair(got))
    value = (value + (pot[...] - center_shift) * field[...]) * (1.0 / half_width)
    current[...] = value
    cells_apply(
        pair(value), k_high[...], k_low[...], c01[...], c10[...], m01[...], local, send
    )


def leave_kernel(sectioned, recv, m23t, pot, current, field, scatter, out):
    got = jnp.concatenate([recv[0], recv[1]], axis=0)
    value = sectioned[...] + select(m23t[...], pair(got))
    value = (value + (pot[...] - center_shift) * current[...]) * (2.0 / half_width) - field[...]
    out[...] = select(scatter[...], pair(value))[: out.shape[0]]


def call(body, out_shapes, *args, scratch=(), flops=0):
    one = not isinstance(out_shapes, (tuple, list))
    shapes = [out_shapes] if one else list(out_shapes)
    size = sum(math.prod(a.shape) * a.dtype.itemsize for a in (*args, *shapes))
    full = lambda a: pl.BlockSpec(memory_space=pltpu.VMEM)
    return pl.pallas_call(
        body,
        out_shape=out_shapes,
        in_specs=[full(a) for a in args],
        out_specs=full(shapes[0]) if one else [full(s) for s in shapes],
        scratch_shapes=list(scratch),
        cost_estimate=pl.CostEstimate(flops=flops, bytes_accessed=size, transcendentals=0),
        compiler_params=pltpu.CompilerParams(vmem_limit_bytes=48 << 20),
    )(*args)


def state_id(y, x, core):
    return (y % SIDE_Y) * (SIDE_X * 2) + (x % SIDE_X) * 2 + core % 2


def shift_state(value, dy, dx, dcore):
    pairs = [
        (state_id(y, x, c), state_id(y + dy, x + dx, c + dcore))
        for y in range(SIDE_Y)
        for x in range(SIDE_X)
        for c in range(2)
    ]
    return lax.ppermute(value, "state", pairs)


def matmul(left, right):
    return jnp.dot(left, right, precision=lax.Precision.HIGH, preferred_element_type=jnp.float32)


def rotate(block, rotation):
    rows, cols = block.shape
    own = lax.axis_index("state")
    y, x, core = own // (SIDE_X * 2), (own // 2) % SIDE_X, own % 2
    chips = rotation.reshape(SIDE_Y * SIDE_X, 2, cols, cols)
    theirs = lax.dynamic_index_in_dim(chips, 1 - core, 1, keepdims=False)
    partner = shift_state(theirs, 0, 0, 1)
    half = rows // 16 * 8

    left = shift_state(block, 0, 1, 0)
    right = shift_state(block, 0, -1, 0)
    across = shift_state(block, 1, 0, 0)
    far_top = shift_state(left[:half], 0, 1, 0)
    far_low = shift_state(right[half:], 0, -1, 0)
    across_left = shift_state(across, 0, 1, 0)
    across_right = shift_state(across, 0, -1, 0)
    across_far_top = shift_state(far_top, 1, 0, 0)
    across_far_low = shift_state(far_low, 1, 0, 0)

    def part(value, dy, dx):
        chip = ((y + dy) % SIDE_Y) * SIDE_X + (x + dx) % SIDE_X
        mine = lax.dynamic_slice_in_dim(rotation, (chip * 2 + core) * cols, cols, 0)
        other = lax.dynamic_index_in_dim(partner, chip, 0, keepdims=False)
        return matmul(value, mine), matmul(value, other)

    def add(a, b):
        return a[0] + b[0], a[1] + b[1]

    total = part(block, 0, 0)
    total = add(total, part(left, 0, -1))
    total = add(total, part(right, 0, 1))
    total = add(total, part(across, 1, 0))
    total = add(total, part(jnp.concatenate([far_top, far_low]), 0, 2))
    total = add(total, part(across_left, 1, -1))
    total = add(total, part(across_right, 1, 1))
    total = add(total, part(jnp.concatenate([across_far_top, across_far_low]), 1, 2))
    return total[0] + shift_state(total[1], 0, 0, 1)


def shift_mesh(value, steps):
    count = lax.axis_size("mesh")
    first, last = (max(0, -steps), min(count, count - steps))
    return lax.ppermute(value, "mesh", [(source, source + steps) for source in range(first, last)])


def f32(*shape):
    return jax.ShapeDtypeStruct(shape, jnp.float32)


def make_tables(stiffness, potential, cell_nodes, shared_rows, shared_count, nodes):
    cells, npc = cell_nodes.shape
    pad = up(npc, 256)
    node_pad = up(nodes, LANES)
    matrix = jnp.pad(stiffness, ((0, pad - npc), (0, pad - npc)))
    high = lax.reduce_precision(matrix, 8, 7)
    k_high, k_low = high.astype(jnp.bfloat16), (matrix - high).astype(jnp.bfloat16)
    down = jnp.pad(cell_nodes, ((0, 0), (0, pad - npc)), constant_values=-1)
    over = jnp.pad(cell_nodes, ((0, 0), (0, pad - npc)), constant_values=-2)
    bf = jnp.bfloat16
    c01 = (down[0][:, None] == over[1][None, :]).astype(bf)
    c10 = (down[1][:, None] == over[0][None, :]).astype(bf)
    places = down.reshape(-1)
    node_ids = jnp.arange(node_pad, dtype=jnp.int32)
    gather = (places[:, None] == node_ids[None, :]).astype(bf)
    again = jnp.any(cell_nodes[1][:, None] == cell_nodes[0][None, :], axis=1)
    first_second = jnp.where(again, -2, cell_nodes[1])
    first_second = jnp.pad(first_second, (0, pad - npc), constant_values=-2)
    first_copy = jnp.concatenate([over[0], first_second])
    out_ids = jnp.arange(up(nodes, 8), dtype=jnp.int32)
    scatter = (out_ids[:, None] == first_copy[None, :]).astype(bf)
    used = jnp.arange(shared_rows.shape[1])[None, :] < shared_count[0][:, None]
    lists = jnp.where(used, shared_rows, -3)
    short = up(NEAR, 8)
    longer = up(shared_rows.shape[1], 8)
    near = jnp.pad(lists[:2, :NEAR], ((0, 0), (0, short - NEAR)), constant_values=-3)
    far = jnp.pad(lists[2:], ((0, 0), (0, longer - shared_rows.shape[1])), constant_values=-3)
    near, far = near.reshape(-1), far.reshape(-1)
    m01 = (near[:, None] == over.reshape(-1)[None, :]).astype(bf)
    m01t = (places[:, None] == near[None, :]).astype(bf)
    m23 = (far[:, None] == first_copy[None, :]).astype(bf)
    m23t = (places[:, None] == far[None, :]).astype(bf)
    potential = jnp.pad(potential, (0, node_pad - nodes))
    per_place = jnp.sum(jnp.where(gather > 0, potential[None, :], 0.0), axis=1, keepdims=True)
    return dict(
        k=(k_high, k_low), c=(c01, c10), gather=gather, scatter=scatter, m01=m01, m01t=m01t,
        m23=m23, m23t=m23t, pot=per_place, short=short, longer=longer, pad=pad, node_pad=node_pad,
    )


def filter_states(values, t, grid_side):
    rows, cols = values.shape
    pad, node_pad, short, longer = t["pad"], t["node_pad"], t["short"], t["longer"]
    places = 2 * pad
    matrices = (*t["k"], *t["c"], t["m01"])

    def trade_near(send):
        return jnp.stack([shift_mesh(send[1], -grid_side), shift_mesh(send[0], grid_side)])

    def trade_far(send):
        return jnp.stack([shift_mesh(send[1], -1), shift_mesh(send[0], 1)])

    near, far = f32(2, short, cols), f32(2, longer, cols)
    whole = f32(places, cols)
    field, local, send = call(
        enter_kernel, (whole, whole, near), values, t["gather"], *matrices,
        scratch=[pltpu.VMEM((node_pad, 2 * cols), jnp.bfloat16)],
    )
    sectioned, send = call(
        middle_kernel, (whole, far), local, trade_near(send), t["m01t"], t["m23"]
    )
    current, local, send = call(
        again_kernel, (whole, whole, near), sectioned, trade_far(send), t["m23t"], t["pot"], field,
        *matrices,
    )
    sectioned, send = call(
        middle_kernel, (whole, far), local, trade_near(send), t["m01t"], t["m23"]
    )
    return call(
        leave_kernel, f32(rows, cols), sectioned, trade_far(send), t["m23t"], t["pot"], current,
        field, t["scatter"],
    )


def per_device(states_in, rotation, stiffness, potential, cell_nodes, shared_rows, shared_count):
    grid_side = math.isqrt(lax.axis_size("mesh"))
    tables = make_tables(
        stiffness[0], potential, cell_nodes, shared_rows, shared_count, states_in.shape[0]
    )
    return filter_states(rotate(states_in, rotation), tables, grid_side)


def solution(mesh):
    return jax.shard_map(
        per_device,
        mesh=mesh,
        in_specs=(
            P("mesh", "state"),
            P(None, "state"),
            P("mesh", None, None),
            P("mesh"),
            P("mesh", None),
            P("mesh", None),
            P("mesh", None),
        ),
        out_specs=P("mesh", "state"),
        check_vma=False,
    )
```
